32 devices in a mesh: ctx: 16 (over z, x, core), head: 2 (over y).
Axes of the slice: x: 2, y: 2, z: 4, core: 2. Of those that a mesh axis runs over, the one named last changes fastest.
Arguments:
- q_latent: bfloat16 [2048, 1536], P(('ctx', 'head')), may hold values from -320 to 320
- q_gain: float32 [1536], replicated, may hold values from 0.5 to 8
- kv_cache: bfloat16 [2048, 576], P(('ctx', 'head')), may hold values from -320 to 320
- kv_gain: float32 [512], replicated, may hold values from 0.5 to 8
- w_query: bfloat16 [1536, 12288], P(None, 'head'), may hold values from -0.15625 to 0.15625
- w_kv: bfloat16 [512, 16384], P(None, 'head'), may hold values from -0.25 to 0.25
- doc_lengths: int32 [3], replicated, may hold values from 1 to 1024, 2048 in all
Outputs:
- attn_out: bfloat16 [2048, 8192], P('ctx', 'head')
The draws below stay inside these ranges and needn't reach their ends.
Inputs may be any that keep to these rules, and one draw needn't show every extreme that they name: `doc_lengths`: 3 documents, lengths in order summing to 2048; the longest has exactly 1024 tokens.
All inputs are finite; a program needn't handle non-finite values.
Results may differ from the reference program's by a relative error of at most 0.0075.
The reference program's roundings to bfloat16 on the way count: a program that leaves them out, or rounds other values in their place, can miss the bound.
Values may be sent and summed in bfloat16 or wider, within the bound.
A program may use at most 192 MiB of HBM per device.

```python
import math
import jax
import jax.numpy as jnp
import numpy as np
from jax import lax

QL = 1536
KL = 512
RD = 64
ND = 128
VD = 128
HEADS = 64
DOCS = 3
SEQ = 2048


def scaled_rows(key, row_count, col_count, plain_cols):
    normal_key = jax.random.fold_in(key, 101)
    row_key = jax.random.fold_in(key, 202)
    col_key = jax.random.fold_in(key, 303)
    values = jax.random.truncated_normal(normal_key, -4.0, 4.0, (row_count, col_count), jnp.float32)
    row_top = math.log(10.0)
    row_scale = jnp.exp(jax.random.uniform(row_key, (row_count, 1), jnp.float32, 0.0, row_top))
    col_scale = jnp.exp(jax.random.uniform(col_key, (1, col_count), jnp.float32, 0.0, math.log(3.0)))
    column_index = jnp.arange(col_count, dtype=jnp.int32)[None, :]
    scaled = values * row_scale * col_scale
    return jnp.where(column_index < col_count - plain_cols, scaled, values)


def gain_values(key, width):
    return jax.random.uniform(key, (width,), jnp.float32, 0.5, 1.5)


def draw_q_latent(key, part):
    return scaled_rows(jax.random.fold_in(key, 11), SEQ, QL, 0).astype(jnp.bfloat16)


def draw_kv_cache(key, part):
    return scaled_rows(jax.random.fold_in(key, 23), SEQ, KL + RD, RD).astype(jnp.bfloat16)


def draw_q_gain(key, part):
    return gain_values(jax.random.fold_in(key, 37), QL)


def draw_kv_gain(key, part):
    return gain_values(jax.random.fold_in(key, 41), KL)


def block_levels(own_key, dims, pieces, smallest, high):
    factor_of = 1.0
    for axis_at, shards_of in pieces:
        draws = jax.random.uniform(jax.random.fold_in(jax.random.fold_in(own_key, 6), axis_at), (shards_of,), jnp.float32, smallest / len(pieces), high / len(pieces))
        factor_of = factor_of * jnp.repeat(jnp.exp(draws), dims[axis_at] // shards_of).reshape((-1,) + (1,) * (len(dims) - 1 - axis_at))
    return factor_of


def split_up(count, total, most, slope):
    loads = [(1 << 20) // math.isqrt(grade ** slope) + 1 for grade in range(2, count + 1)]
    surplus, holding = total - most - (count - 1), [1] * (count - 1)
    while surplus > 0:
        movable = [i for i in range(count - 1) if holding[i] < most]
        whole, budget = sum([loads[i] for i in movable]), surplus
        for i in movable:
            more = min(most - holding[i], max(1, budget * loads[i] // whole), surplus)
            holding[i] = holding[i] + more
            surplus = surplus - more
    return np.array([most] + holding)


def ragged(own_key, count, total, reach, slope):
    if count == 2:
        one = jax.random.randint(own_key, (), max(1, total - reach), min(reach, total - 1) + 1)
        return jnp.stack([one, total - one])
    sizes = jnp.asarray(split_up(count, total, reach, slope), jnp.int32)
    pairs = (count - 1) // 2
    source_of, receiver = sizes[1:1 + 2 * pairs:2], sizes[2:2 + 2 * pairs:2]
    slack = jnp.minimum(source_of - 1, reach - receiver)
    moved = jax.random.randint(jax.random.fold_in(own_key, 1), (pairs,), 0, 1 << 20) % (slack + 1)
    sizes = sizes.at[1:1 + 2 * pairs:2].set(source_of - moved).at[2:2 + 2 * pairs:2].set(receiver + moved)
    return sizes[jax.random.permutation(jax.random.fold_in(own_key, 2), count)]


def normal_values(own_key, dims, scale, reach, pieces=(), kind=jnp.bfloat16):
    level = block_levels(own_key, dims, pieces, -0.22, 0.18) if pieces else 1.0
    entries = jax.random.normal(own_key, dims, jnp.float32) * scale * level
    return jnp.minimum(jnp.maximum(entries, -reach), reach).astype(kind)


def setup_inputs(seed: int = 0) -> dict:
    streams_of = jax.random.split(jax.random.key(seed), 8)
    return {
        "q_latent": draw_q_latent(jax.random.fold_in(streams_of[7], 71), 0),
        "q_gain": draw_q_gain(jax.random.fold_in(streams_of[7], 71), 0),
        "kv_cache": draw_kv_cache(jax.random.fold_in(streams_of[7], 71), 0),
        "kv_gain": draw_kv_gain(jax.random.fold_in(streams_of[7], 71), 0),
        "w_query": normal_values(streams_of[4], (QL, HEADS * (ND + RD)), QL ** -0.5, 0.15625, ((1, 2),)),
        "w_kv": normal_values(streams_of[5], (KL, HEADS * (ND + VD)), KL ** -0.5, 0.25, ((1, 2),)),
        "doc_lengths": ragged(streams_of[6], DOCS, SEQ, SEQ // 2, 0).astype(jnp.int32),
    }


epsilon = 1e-06

def rms_scale(rows, gain):
    values = rows.astype(jnp.float32)
    return values * lax.rsqrt(lax.optimization_barrier(jnp.mean(values * values, axis=-1, keepdims=True)) + epsilon) * gain

def doc_tables(doc_lengths, positions):
    doc_ends = jnp.cumsum(doc_lengths).astype(jnp.int32)
    passed = positions[:, None] >= doc_ends[None, :]
    doc_index = lax.optimization_barrier(jnp.sum(passed.astype(jnp.int32), axis=1)).astype(jnp.int32)
    doc_start = lax.optimization_barrier(jnp.sum(jnp.where(passed, doc_lengths[None, :], 0), axis=1)).astype(jnp.int32)
    return (doc_index, doc_start)

def rotate_pairs(values, offsets):
    half_width = values.shape[-1] // 2
    freq_index = jnp.arange(half_width, dtype=jnp.float32)
    frequency = jnp.exp(freq_index * (-2.0 * math.log(10000.0) / values.shape[-1]))
    angles = offsets.astype(jnp.float32)[:, None] * frequency[None, :]
    cosine = jnp.cos(angles)[:, None, :]
    sine_part = jnp.sin(angles)[:, None, :]
    lower_half = values[..., :half_width]
    upper_half = values[..., half_width:]
    return jnp.concatenate([lower_half * cosine - upper_half * sine_part, upper_half * cosine + lower_half * sine_part], axis=-1)

def project_queries(latent_rows, q_gain, w_query, offsets, nope_width, rope_width):
    normed = rms_scale(latent_rows, q_gain).astype(jnp.bfloat16)
    projected = jnp.dot(normed, w_query, preferred_element_type=jnp.float32)
    head_count = w_query.shape[1] // (nope_width + rope_width)
    projected = projected.reshape(latent_rows.shape[0], head_count, nope_width + rope_width)
    rotated = rotate_pairs(projected[..., nope_width:], offsets)
    return jnp.concatenate([projected[..., :nope_width], rotated], axis=-1).astype(jnp.bfloat16)

def reference(q_latent, q_gain, kv_cache, kv_gain, w_query, w_kv, doc_lengths):
    positions = jnp.arange(SEQ, dtype=jnp.int32)
    doc_index, doc_start = doc_tables(doc_lengths, positions)
    queries = project_queries(q_latent, q_gain, w_query, positions - doc_start, ND, RD)
    kv_normed = rms_scale(kv_cache[:, :KL], kv_gain).astype(jnp.bfloat16)
    expanded = jnp.dot(kv_normed, w_kv, preferred_element_type=jnp.float32).astype(jnp.bfloat16)
    expanded = expanded.reshape(SEQ, HEADS, ND + VD)
    key_rope = kv_cache[:, KL:]
    block_size = min(512, SEQ)
    window = min(SEQ, SEQ // 2 + block_size)
    score_scale = 1.0 / math.sqrt(ND + RD)

    def one_block(number):
        first_row = (number * block_size).astype(jnp.int32)
        key_first = jnp.clip(first_row + block_size - window, 0, SEQ - window).astype(jnp.int32)
        query_block = lax.dynamic_slice_in_dim(queries, first_row, block_size, 0).astype(jnp.float32)
        key_block = lax.dynamic_slice_in_dim(expanded, key_first, window, 0).astype(jnp.float32)
        rope_block = lax.dynamic_slice_in_dim(key_rope, key_first, window, 0).astype(jnp.float32)
        scores = jnp.einsum('qhd,khd->hqk', query_block[..., :ND], key_block[..., :ND])
        scores = (scores + jnp.einsum('qhr,kr->hqk', query_block[..., ND:], rope_block)) * score_scale
        query_pos = first_row + jnp.arange(block_size, dtype=jnp.int32)
        key_pos = key_first + jnp.arange(window, dtype=jnp.int32)
        query_doc = lax.dynamic_slice_in_dim(doc_index, first_row, block_size, 0)
        key_doc = lax.dynamic_slice_in_dim(doc_index, key_first, window, 0)
        allowed = (key_pos[None, :] <= query_pos[:, None]) & (key_doc[None, :] == query_doc[:, None])
        masked = jnp.where(allowed[None], scores, -1e+30)
        running_max = lax.optimization_barrier(jnp.max(masked, axis=-1))
        weights = jnp.where(allowed[None], jnp.exp(scores - running_max[..., None]), 0.0)
        row_total = lax.optimization_barrier(jnp.sum(weights, axis=-1))
        rounded = lax.optimization_barrier(weights.astype(jnp.bfloat16))
        mixed = jnp.einsum('hqk,khv->qhv', rounded.astype(jnp.float32), key_block[..., ND:])
        mixed = mixed / jnp.transpose(row_total)[:, :, None]
        return mixed.reshape(block_size, HEADS * VD)
    outputs = lax.map(one_block, jnp.arange(SEQ // block_size, dtype=jnp.int32))
    return outputs.reshape(SEQ, HEADS * VD).astype(jnp.bfloat16)
```

```python
import functools
import math

import jax
import jax.numpy as jnp
from jax import lax
from jax.experimental import pallas as pl
from jax.experimental.pallas import tpu as pltpu
from jax.sharding import PartitionSpec as P

KL = 512
RD = 64
ND = 128
VD = 128
MESH = pl.DeviceIdType.MESH

epsilon = 1e-06


def gather_kernel(nc, nh, q_ref, kv_ref, qall_ref, win_ref, q_send, q_recv, a_send, a_recv, b_send, b_recv, c_send, c_recv):
    c = lax.axis_index("ctx")
    h = lax.axis_index("head")
    rows = kv_ref.shape[0]
    back = nc // 2
    half = back // 2
    par = lax.rem(c, 2)
    other = c + 1 - 2 * par
    head_of = [lax.rem(h + k, nh) for k in range(nh)]

    def part(slot, head):
        return win_ref.at[slot, pl.ds(pl.multiple_of(head * rows, rows), rows)]

    def qpart(head):
        return qall_ref.at[pl.ds(pl.multiple_of(head * rows, rows), rows)]

    def remote(src, dst, send, recv, ctx, head):
        return pltpu.make_async_remote_copy(
            src_ref=src, dst_ref=dst, send_sem=send, recv_sem=recv, device_id=(ctx, head), device_id_type=MESH
        )

    barrier = pltpu.get_barrier_semaphore()

    def greet(ctx, head):
        pl.semaphore_signal(barrier, inc=1, device_id=(ctx, head), device_id_type=MESH)

    for k in range(1, nh):
        greet(c, head_of[k])
    greet(other, h)
    for j in range(1, nc // 2):
        greet(lax.rem(c + 2 * j, nc), h)
    pl.semaphore_wait(barrier, nh + nc // 2 - 1)

    def q_copy(k):
        return remote(q_ref, qpart(h), q_send.at[k - 1], q_recv.at[k - 1], c, head_of[k])

    def a_copy(j):
        return remote(kv_ref, part(back - 2 * j, h), a_send.at[j - 1], a_recv.at[j - 1], c + 2 * j, h)

    def b_copy(j, k):
        src = kv_ref if j == 0 else part(back - 2 * j, h)
        return remote(src, part(back - 2 * j, h), b_send.at[j, k - 1], b_recv.at[j, k - 1], c, head_of[k])

    def c_copy(t, k, src=None):
        head = head_of[0] if k == 0 else head_of[nh - k]
        src = part(back - 2 * t - 2 * par, head) if src is None else src
        return remote(src, part(back - 2 * t - 1, head), c_send.at[t, k], c_recv.at[t, k], other, h)

    for j in range(1, half + 1):
        pl.when(c + 2 * j < nc)(lambda j=j: a_copy(j).start())
    for k in range(1, nh):
        b_copy(0, k).start()
        q_copy(k).start()

    @pl.when(par == 0)
    def _():
        c_copy(0, 0, kv_ref).start()

    win_ref[back, pl.ds(pl.multiple_of(h * rows, rows), rows)] = kv_ref[...]
    qall_ref[pl.ds(pl.multiple_of(h * rows, rows), rows)] = q_ref[...]
    for slot in range(back):
        @pl.when(c - back + slot < 0)
        def _(slot=slot):
            win_ref[slot] = jnp.zeros(win_ref.shape[1:], win_ref.dtype)

    def forward(j, k):
        if j < half:
            @pl.when(par == 0)
            def _():
                c_copy(j, k).start()
        if j > 0:
            @pl.when(par == 1)
            def _():
                c_copy(j - 1, k).start()

    for k in range(1, nh):
        b_copy(0, k).wait_recv()
        forward(0, k)
    for j in range(1, half + 1):
        @pl.when(c - 2 * j >= 0)
        def _(j=j):
            a_copy(j).wait_recv()
            for k in range(1, nh):
                b_copy(j, k).start()
            forward(j, 0)
    for j in range(1, half + 1):
        @pl.when(c - 2 * j >= 0)
        def _(j=j):
            for k in range(1, nh):
                b_copy(j, k).wait_recv()
                forward(j, k)
    for k in range(1, nh):
        q_copy(k).wait_recv()
    for t in range(half):
        @pl.when(c - 2 * t - 1 >= 0)
        def _(t=t):
            for k in range(nh):
                c_copy(t, k).wait_recv()
    for k in range(1, nh):
        q_copy(k).wait_send()
        b_copy(0, k).wait_send()
    for j in range(1, half + 1):
        pl.when(c + 2 * j < nc)(lambda j=j: a_copy(j).wait_send())

        @pl.when(c - 2 * j >= 0)
        def _(j=j):
            for k in range(1, nh):
                b_copy(j, k).wait_send()
    for t in range(half):
        @pl.when(c - 2 * t - 2 * par >= 0)
        def _(t=t):
            for k in range(nh):
                c_copy(t, k).wait_send()


def gather(q_latent, kv_cache, nc, nh):
    rows, ql = q_latent.shape
    width = kv_cache.shape[1]
    back = nc // 2
    half = back // 2
    peers = max(nh - 1, 1)
    dma = pltpu.SemaphoreType.DMA
    vmem = pl.BlockSpec(memory_space=pltpu.VMEM)
    return pl.pallas_call(
        functools.partial(gather_kernel, nc, nh),
        out_shape=(
            jax.ShapeDtypeStruct((nh * rows, ql), q_latent.dtype),
            jax.ShapeDtypeStruct((back + 1, nh * rows, width), kv_cache.dtype),
        ),
        in_specs=[vmem, vmem],
        out_specs=(vmem, vmem),
        scratch_shapes=[
            dma((peers,)), dma((peers,)), dma((half,)), dma((half,)),
            dma((half + 1, peers)), dma((half + 1, peers)), dma((half, nh)), dma((half, nh)),
        ],
        compiler_params=pltpu.CompilerParams(collective_id=0, has_side_effects=True),
        name="gather",
    )(q_latent, kv_cache)


def normed(values, gain):
    values = values.astype(jnp.float32)
    mean = jnp.mean(values * values, axis=-1, keepdims=True)
    return (values * lax.rsqrt(mean + epsilon) * gain).astype(jnp.bfloat16)


def attend_kernel(heads, first_ref, len_ref, q_ref, qg_ref, win_ref, kvg_ref, wq_ref, wkv_ref, out_ref, qn, kvn, kr, bias, cos, sin):
    tok = q_ref.shape[0]
    keys = win_ref.shape[0]
    docs = len_ref.shape[0]

    @pl.when(pl.program_id(0) == 0)
    def _():
        first = first_ref[0]
        qn[...] = normed(q_ref[...], qg_ref[...])
        kvn[...] = normed(win_ref[:, :KL], kvg_ref[...])
        kr[...] = win_ref[:, KL:]

        def start_of(pos):
            start = jnp.zeros_like(pos)
            end = jnp.int32(0)
            for d in range(docs):
                end = end + len_ref[d]
                start = start + jnp.where(pos >= end, len_ref[d], 0)
            return start

        qpos = first + lax.broadcasted_iota(jnp.int32, (tok, keys), 0)
        kpos = first - (keys - tok) + lax.broadcasted_iota(jnp.int32, (tok, keys), 1)
        allowed = (kpos <= qpos) & (kpos >= start_of(qpos))
        bias[...] = jnp.where(allowed, 0.0, -1e30)
        pos = first + lax.broadcasted_iota(jnp.int32, (tok, RD), 0)
        lane = lax.broadcasted_iota(jnp.int32, (tok, RD), 1)
        freq_index = jnp.where(lane < RD // 2, lane, lane - RD // 2).astype(jnp.float32)
        frequency = jnp.exp(freq_index * (-2.0 * math.log(10000.0) / RD))
        angles = (pos - start_of(pos)).astype(jnp.float32) * frequency
        cos[...] = jnp.cos(angles)
        sine = jnp.sin(angles)
        sin[...] = jnp.where(lane < RD // 2, -sine, sine)

    scale = math.log2(math.e) / math.sqrt(ND + RD)
    made = jnp.dot(qn[...], wq_ref[...], preferred_element_type=jnp.float32)
    for n in range(heads):
        at = n * (ND + RD)
        turn = made[:, at + ND : at + ND + RD]
        swapped = jnp.concatenate([turn[:, RD // 2 :], turn[:, : RD // 2]], axis=1)
        turn = turn * cos[...] + swapped * sin[...]
        query = jnp.concatenate([made[:, at : at + ND], turn], axis=1).astype(jnp.bfloat16)
        at = n * (ND + VD)
        expanded = jnp.dot(
            kvn[...], wkv_ref[:, at : at + ND + VD], preferred_element_type=jnp.float32
        ).astype(jnp.bfloat16)
        key = jnp.concatenate([expanded[:, :ND], kr[...]], axis=1)
        scores = lax.dot_general(query, key, (((1,), (1,)), ((), ())), preferred_element_type=jnp.float32)
        scores = scores + bias[...]
        top = jnp.max(scores, axis=1, keepdims=True)
        weights = jnp.exp2((scores - top) * scale)
        total = jnp.sum(weights, axis=1, keepdims=True)
        mixed = jnp.dot(weights.astype(jnp.bfloat16), expanded[:, ND:], preferred_element_type=jnp.float32)
        out_ref[:, n * VD : (n + 1) * VD] = (mixed / total).astype(jnp.bfloat16)


def attend(first, doc_lengths, q_rows, q_gain, window, kv_gain, w_query, w_kv, heads):
    tok, ql = q_rows.shape
    keys, width = window.shape
    all_heads = w_query.shape[1] // (ND + RD)
    whole = lambda shape: pl.BlockSpec(shape, lambda i, *refs: (0, 0))
    return pl.pallas_call(
        functools.partial(attend_kernel, heads),
        out_shape=jax.ShapeDtypeStruct((tok, all_heads * VD), jnp.bfloat16),
        grid_spec=pltpu.PrefetchScalarGridSpec(
            num_scalar_prefetch=2,
            grid=(all_heads // heads,),
            in_specs=[
                whole((tok, ql)),
                whole((1, ql)),
                whole((keys, width)),
                whole((1, KL)),
                pl.BlockSpec((ql, heads * (ND + RD)), lambda i, *refs: (0, i)),
                pl.BlockSpec((KL, heads * (ND + VD)), lambda i, *refs: (0, i)),
            ],
            out_specs=pl.BlockSpec((tok, heads * VD), lambda i, *refs: (0, i)),
            scratch_shapes=[
                pltpu.VMEM((tok, ql), jnp.bfloat16),
                pltpu.VMEM((keys, KL), jnp.bfloat16),
                pltpu.VMEM((keys, RD), jnp.bfloat16),
                pltpu.VMEM((tok, keys), jnp.float32),
                pltpu.VMEM((tok, RD), jnp.float32),
                pltpu.VMEM((tok, RD), jnp.float32),
            ],
        ),
        compiler_params=pltpu.CompilerParams(
            dimension_semantics=("arbitrary",), vmem_limit_bytes=60 * 2**20
        ),
        name="attend",
    )(first, doc_lengths, q_rows, q_gain, window, kv_gain, w_query, w_kv)


def solution(mesh):
    nc, nh = mesh.shape["ctx"], mesh.shape["head"]

    def body(q_latent, q_gain, kv_cache, kv_gain, w_query, w_kv, doc_lengths):
        q_rows, window = gather(q_latent, kv_cache, nc, nh)
        first = (lax.axis_index("ctx") * q_rows.shape[0]).astype(jnp.int32).reshape(1)
        window = window.reshape(-1, window.shape[-1])
        return attend(first, doc_lengths, q_rows, q_gain[None], window, kv_gain[None], w_query, w_kv, 4)

    placed = (
        P(("ctx", "head"), None),
        P(),
        P(("ctx", "head"), None),
        P(),
        P(None, "head"),
        P(None, "head"),
        P(),
    )
    return jax.shard_map(body, mesh=mesh, in_specs=placed, out_specs=P("ctx", "head"), check_vma=False)
```

```python
import functools
import math

import jax
import jax.numpy as jnp
from jax import lax
from jax.experimental import pallas as pl
from jax.experimental.pallas import tpu as pltpu
from jax.sharding import PartitionSpec as P

KL = 512
RD = 64
ND = 128
VD = 128
MESH = pl.DeviceIdType.MESH

epsilon = 1e-06


def gather_kernel(nc, nh, q_ref, kv_ref, qall_ref, win_ref, q_send, q_recv, a_send, a_recv, b_send, b_recv, c_send, c_recv):
    c = lax.axis_index("ctx")
    h = lax.axis_index("head")
    rows = kv_ref.shape[0]
    back = nc // 2
    half = back // 2
    par = lax.rem(c, 2)
    other = c + 1 - 2 * par
    head_of = [lax.rem(h + k, nh) for k in range(nh)]

    def part(slot, head):
        return win_ref.at[slot, pl.ds(pl.multiple_of(head * rows, rows), rows)]

    def qpart(head):
        return qall_ref.at[pl.ds(pl.multiple_of(head * rows, rows), rows)]

    def remote(src, dst, send, recv, ctx, head):
        return pltpu.make_async_remote_copy(
            src_ref=src, dst_ref=dst, send_sem=send, recv_sem=recv, device_id=(ctx, head), device_id_type=MESH
        )

    barrier = pltpu.get_barrier_semaphore()

    def greet(ctx, head):
        pl.semaphore_signal(barrier, inc=1, device_id=(ctx, head), device_id_type=MESH)

    for k in range(1, nh):
        greet(c, head_of[k])
    greet(other, h)
    for j in range(1, nc // 2):
        greet(lax.rem(c + 2 * j, nc), h)
    pl.semaphore_wait(barrier, nh + nc // 2 - 1)

    def q_copy(k):
        return remote(q_ref, qpart(h), q_send.at[k - 1], q_recv.at[k - 1], c, head_of[k])

    def a_copy(j):
        return remote(kv_ref, part(back - 2 * j, h), a_send.at[j - 1], a_recv.at[j - 1], c + 2 * j, h)

    def b_copy(j, k):
        src = kv_ref if j == 0 else part(back - 2 * j, h)
        return remote(src, part(back - 2 * j, h), b_send.at[j, k - 1], b_recv.at[j, k - 1], c, head_of[k])

    def c_copy(t, k, src=None):
        head = head_of[0] if k == 0 else head_of[nh - k]
        src = part(back - 2 * t - 2 * par, head) if src is None else src
        return remote(src, part(back - 2 * t - 1, head), c_send.at[t, k], c_recv.at[t, k], other, h)

    for j in range(1, half + 1):
        pl.when(c + 2 * j < nc)(lambda j=j: a_copy(j).start())
    for k in range(1, nh):
        b_copy(0, k).start()
        q_copy(k).start()

    @pl.when(par == 0)
    def _():
        c_copy(0, 0, kv_ref).start()

    win_ref[back, pl.ds(pl.multiple_of(h * rows, rows), rows)] = kv_ref[...]
    qall_ref[pl.ds(pl.multiple_of(h * rows, rows), rows)] = q_ref[...]
    for slot in range(back):
        @pl.when(c - back + slot < 0)
        def _(slot=slot):
            win_ref[slot] = jnp.zeros(win_ref.shape[1:], win_ref.dtype)

    def forward(j, k):
        if j < half:
            @pl.when(par == 0)
            def _():
                c_copy(j, k).start()
        if j > 0:
            @pl.when(par == 1)
            def _():
                c_copy(j - 1, k).start()

    for k in range(1, nh):
        b_copy(0, k).wait_recv()
        forward(0, k)
    for j in range(1, half + 1):
        @pl.when(c - 2 * j >= 0)
        def _(j=j):
            a_copy(j).wait_recv()
            for k in range(1, nh):
                b_copy(j, k).start()
            forward(j, 0)
    for j in range(1, half + 1):
        @pl.when(c - 2 * j >= 0)
        def _(j=j):
            for k in range(1, nh):
                b_copy(j, k).wait_recv()
                forward(j, k)
    for k in range(1, nh):
        q_copy(k).wait_recv()
    for t in range(half):
        @pl.when(c - 2 * t - 1 >= 0)
        def _(t=t):
            for k in range(nh):
                c_copy(t, k).wait_recv()
    for k in range(1, nh):
        q_copy(k).wait_send()
        b_copy(0, k).wait_send()
    for j in range(1, half + 1):
        pl.when(c + 2 * j < nc)(lambda j=j: a_copy(j).wait_send())

        @pl.when(c - 2 * j >= 0)
        def _(j=j):
            for k in range(1, nh):
                b_copy(j, k).wait_send()
    for t in range(half):
        @pl.when(c - 2 * t - 2 * par >= 0)
        def _(t=t):
            for k in range(nh):
                c_copy(t, k).wait_send()


def gather(q_latent, kv_cache, nc, nh):
    rows, ql = q_latent.shape
    width = kv_cache.shape[1]
    back = nc // 2
    half = back // 2
    peers = max(nh - 1, 1)
    dma = pltpu.SemaphoreType.DMA
    vmem = pl.BlockSpec(memory_space=pltpu.VMEM)
    return pl.pallas_call(
        functools.partial(gather_kernel, nc, nh),
        out_shape=(
            jax.ShapeDtypeStruct((nh * rows, ql), q_latent.dtype),
            jax.ShapeDtypeStruct((back + 1, nh * rows, width), kv_cache.dtype),
        ),
        in_specs=[vmem, vmem],
        out_specs=(vmem, vmem),
        scratch_shapes=[
            dma((peers,)), dma((peers,)), dma((half,)), dma((half,)),
            dma((half + 1, peers)), dma((half + 1, peers)), dma((half, nh)), dma((half, nh)),
        ],
        compiler_params=pltpu.CompilerParams(collective_id=0, has_side_effects=True),
        name="gather",
    )(q_latent, kv_cache)


def normed(values, gain):
    values = values.astype(jnp.float32)
    mean = jnp.mean(values * values, axis=-1, keepdims=True)
    return (values * lax.rsqrt(mean + epsilon) * gain).astype(jnp.bfloat16)


def attend_kernel(heads, first_ref, len_ref, q_ref, qg_ref, win_ref, kvg_ref, wq_ref, wkv_ref, out_ref, qn, kvn, kr, bias, cos, sin):
    tok = q_ref.shape[0]
    keys = win_ref.shape[0]
    docs = len_ref.shape[0]

    @pl.when(pl.program_id(0) == 0)
    def _():
        first = first_ref[0]
        qn[...] = normed(q_ref[...], qg_ref[...][None])
        kvn[...] = normed(win_ref[:, :KL], kvg_ref[...])
        kr[...] = win_ref[:, KL:]

        def start_of(pos):
            start = jnp.zeros_like(pos)
            end = jnp.int32(0)
            for d in range(docs):
                end = end + len_ref[d]
                start = start + jnp.where(pos >= end, len_ref[d], 0)
            return start

        qpos = first + lax.broadcasted_iota(jnp.int32, (tok, keys), 0)
        kpos = first - (keys - tok) + lax.broadcasted_iota(jnp.int32, (tok, keys), 1)
        allowed = (kpos <= qpos) & (kpos >= start_of(qpos))
        bias[...] = jnp.where(allowed, 0.0, -1e30)
        pos = first + lax.broadcasted_iota(jnp.int32, (tok, RD), 0)
        lane = lax.broadcasted_iota(jnp.int32, (tok, RD), 1)
        freq_index = jnp.where(lane < RD // 2, lane, lane - RD // 2).astype(jnp.float32)
        frequency = jnp.exp(freq_index * (-2.0 * math.log(10000.0) / RD))
        angles = (pos - start_of(pos)).astype(jnp.float32) * frequency
        cos[...] = jnp.cos(angles)
        sine = jnp.sin(angles)
        sin[...] = jnp.where(lane < RD // 2, -sine, sine)

    scale = math.log2(math.e) / math.sqrt(ND + RD)
    made = jnp.dot(qn[...], wq_ref[...], preferred_element_type=jnp.float32)

    def query_of(n):
        at = n * (ND + RD)
        turn = made[:, at + ND : at + ND + RD]
        swapped = jnp.concatenate([turn[:, RD // 2 :], turn[:, : RD // 2]], axis=1)
        turn = turn * cos[...] + swapped * sin[...]
        return jnp.concatenate([made[:, at : at + ND], turn], axis=1).astype(jnp.bfloat16)

    def expand(n):
        at = n * (ND + VD)
        return jnp.dot(
            kvn[...], wkv_ref[:, at : at + ND + VD], preferred_element_type=jnp.float32
        ).astype(jnp.bfloat16)

    def score(query, expanded):
        key = jnp.concatenate([expanded[:, :ND], kr[...]], axis=1)
        scores = lax.dot_general(query, key, (((1,), (1,)), ((), ())), preferred_element_type=jnp.float32)
        return scores + bias[...]

    expanded = [expand(n) for n in range(heads)]
    scores = [score(query_of(n), expanded[n]) for n in range(heads)]
    for n in range(heads):
        top = jnp.max(scores[n], axis=1, keepdims=True)
        weights = jnp.exp2((scores[n] - top) * scale)
        total = jnp.sum(weights, axis=1, keepdims=True)
        mixed = jnp.dot(weights.astype(jnp.bfloat16), expanded[n][:, ND:], preferred_element_type=jnp.float32)
        out_ref[:, n * VD : (n + 1) * VD] = (mixed / total).astype(jnp.bfloat16)


def attend(first, doc_lengths, q_rows, q_gain, window, kv_gain, w_query, w_kv, heads):
    tok, ql = q_rows.shape
    keys, width = window.shape
    all_heads = w_query.shape[1] // (ND + RD)
    whole = lambda shape: pl.BlockSpec(shape, lambda i, *refs: (0, 0))
    return pl.pallas_call(
        functools.partial(attend_kernel, heads),
        out_shape=jax.ShapeDtypeStruct((tok, all_heads * VD), jnp.bfloat16),
        grid_spec=pltpu.PrefetchScalarGridSpec(
            num_scalar_prefetch=2,
            grid=(all_heads // heads,),
            in_specs=[
                whole((tok, ql)),
                pl.BlockSpec((ql,), lambda i, *refs: (0,)),
                whole((keys, width)),
                whole((1, KL)),
                pl.BlockSpec((ql, heads * (ND + RD)), lambda i, *refs: (0, i)),
                pl.BlockSpec((KL, heads * (ND + VD)), lambda i, *refs: (0, i)),
            ],
            out_specs=pl.BlockSpec((tok, heads * VD), lambda i, *refs: (0, i)),
            scratch_shapes=[
                pltpu.VMEM((tok, ql), jnp.bfloat16),
                pltpu.VMEM((keys, KL), jnp.bfloat16),
                pltpu.VMEM((keys, RD), jnp.bfloat16),
                pltpu.VMEM((tok, keys), jnp.float32),
                pltpu.VMEM((tok, RD), jnp.float32),
                pltpu.VMEM((tok, RD), jnp.float32),
            ],
        ),
        compiler_params=pltpu.CompilerParams(
            dimension_semantics=("arbitrary",), vmem_limit_bytes=60 * 2**20
        ),
        name="attend",
    )(first, doc_lengths, q_rows, q_gain, window, kv_gain, w_query, w_kv)


def solution(mesh):
    nc, nh = mesh.shape["ctx"], mesh.shape["head"]

    def body(q_latent, q_gain, kv_cache, kv_gain, w_query, w_kv, doc_lengths):
        q_rows, window = gather(q_latent, kv_cache, nc, nh)
        first = (lax.axis_index("ctx") * q_rows.shape[0]).astype(jnp.int32).reshape(1)
        window = window.reshape(-1, window.shape[-1])
        return attend(first, doc_lengths, q_rows, q_gain, window, kv_gain[None], w_query, w_kv, 4)

    placed = (
        P(("ctx", "head"), None),
        P(),
        P(("ctx", "head"), None),
        P(),
        P(None, "head"),
        P(None, "head"),
        P(),
    )
    return jax.shard_map(body, mesh=mesh, in_specs=placed, out_specs=P("ctx", "head"), check_vma=False)
```
